256 devices in a mesh: dir: 8 (over x_hi, y), space: 32 (over z, x_lo, core).
Axes of the slice: x: 4 (x_hi: 2, x_lo: 2; x = x_hi * 2 + x_lo), y: 4, z: 8, core: 2. Of those that a mesh axis runs over, the one named last changes fastest.
Arguments:
- directions: float32 [16, 2048, 4096], P('dir', 'space'), may hold values from -6.3 to 6.3
- pool: float32 [16, 2048, 4096], P('dir', 'space'), may hold values from -6 to 6
- owners: int32 [2, 2], replicated, may hold values from 0 to 15, as said below
- window_steps: int32 [2], replicated, may hold values from 0 to 511
- diffusion: float32 [512], replicated, may hold values from 0.02 to 0.2
- obs_weight: float32 [2048, 4096], P('space'), may hold values from 0.5 to 2
- prior_diag: float32 [2048, 4096], P('space'), may hold values from 0.1 to 1
Outputs:
- product: float32 [16, 2048, 4096], P('dir', 'space')
- curvature: float32 [16], P('dir')
The draws below stay inside these ranges and needn't reach their ends.
Inputs may be any that keep to these rules, and one draw needn't show every extreme that they name: `owners`: the 4 entries are distinct; 0 and 15 are always among them.
All inputs are finite; a program needn't handle non-finite values.
Results may differ from the reference program's by a relative error of at most 0.00002.
Values sent between devices are 32-bit elements; how exact they have to be, the bound alone decides.
No kernel may reach another device: no remote copies, remote signals or barrier semaphores. Data moves between devices by JAX's collectives and lax.ppermute only.
A program may use at most 64 MiB of HBM per device.

```python
import math
import jax
import jax.numpy as jnp
from jax import lax

COLS = 4096
STEPS = 2
TOTAL_STEPS = 512
NROWS = 2048
DIRS = 16
SLOTS = 16


def draw_owners(key, part):
    first_key, second_key = jax.random.split(jax.random.fold_in(key, 11))
    middle = (jax.random.permutation(first_key, SLOTS - 2) + 1).astype(jnp.int32)
    chosen = jnp.concatenate([jnp.array([0, SLOTS - 1], jnp.int32), middle[:2 * STEPS - 2]])
    shuffle = jax.random.permutation(second_key, 2 * STEPS)
    return chosen[shuffle].reshape(2, STEPS)


def draw_directions(key, part):
    row_place = jnp.arange(NROWS, dtype=jnp.float32)
    row_scale = 0.6 * (1.0 + 2.0 * row_place / max(NROWS - 1, 1))
    base = jnp.clip(jax.random.normal(key, (DIRS, NROWS, COLS), jnp.float32), -3.5, 3.5)
    return base * row_scale[None, :, None]


def shard_levels(rng, shape, shards, least, top_value):
    gain = 1.0
    for position, parts in shards:
        draws = jax.random.uniform(jax.random.fold_in(jax.random.fold_in(rng, 6), position), (parts,), jnp.float32, least / len(shards), top_value / len(shards))
        gain = gain * jnp.repeat(jnp.exp(draws), shape[position] // parts).reshape((-1,) + (1,) * (len(shape) - 1 - position))
    return gain


def noise(stream_key, shape, deviation, bound, cuts=(), kind=jnp.bfloat16):
    values = deviation * jax.random.normal(stream_key, shape, jnp.float32)
    if cuts:
        values = values * shard_levels(stream_key, shape, cuts, -0.22, 0.18)
    return jnp.clip(values, -bound, bound).astype(kind)


def setup_inputs(seed: int = 0) -> dict:
    splits = jax.random.split(jax.random.key(seed), 8)
    return {
        "directions": draw_directions(jax.random.fold_in(splits[7], 71), 0),
        "pool": noise(splits[1], (SLOTS, NROWS, COLS), 1.0, 6.0, ((0, 8), (1, 32)), jnp.float32),
        "owners": draw_owners(jax.random.fold_in(splits[7], 71), 0),
        "window_steps": jax.random.randint(splits[3], (STEPS,), 0, TOTAL_STEPS).astype(jnp.int32),
        "diffusion": jnp.clip(jnp.exp(jax.random.uniform(splits[4], (TOTAL_STEPS,), jnp.float32, math.log(0.02), math.log(0.2))), 0.02, 0.2),
        "obs_weight": jnp.clip(jnp.exp(math.log(2.0) - 1.3862944 * jax.random.uniform(splits[5], (NROWS, COLS), jnp.float32) ** shard_levels(splits[5], (NROWS, COLS), ((0, 32),), -0.2, 0.2)), 0.5, 2.0),
        "prior_diag": jnp.clip(jnp.exp(math.log(1.0) - 2.3025851 * jax.random.uniform(splits[6], (NROWS, COLS), jnp.float32) ** shard_levels(splits[6], (NROWS, COLS), ((0, 32),), -0.2, 0.2)), 0.1, 1.0),
    }


advection_rate = 0.25


def stencil_parts(padded):
    widened = jnp.pad(padded, [(0, 0)] * (padded.ndim - 1) + [(1, 1)])
    centre = widened[..., 1:-1, 1:-1]
    row_above = widened[..., 2:, 1:-1]
    row_below = widened[..., :-2, 1:-1]
    col_right = widened[..., 1:-1, 2:]
    col_left = widened[..., 1:-1, :-2]
    laplace = row_above + row_below + col_right + col_left - 4.0 * centre
    central = 0.5 * (row_above - row_below + col_right - col_left)
    return laplace, central


def rows_padded(values):
    return jnp.pad(values, ((1, 1), (0, 0)))


def reference(directions, pool, owners, window_steps, diffusion, obs_weight, prior_diag):
    rate_list = diffusion[window_steps]
    velocity = [lax.dynamic_index_in_dim(pool, owners[0, moment], 0, keepdims=False) for moment in range(STEPS)]
    adjoint_state = [lax.dynamic_index_in_dim(pool, owners[1, moment], 0, keepdims=False) for moment in range(STEPS)]
    state_slope = [stencil_parts(rows_padded(adjoint_state[moment]))[1] for moment in range(STEPS)]

    def one_probe(probe):
        current = probe
        history = []
        for moment in range(STEPS):
            history.append(current)
            diffused = stencil_parts(rows_padded(current))[0]
            advected = stencil_parts(rows_padded(velocity[moment] * current))[1]
            current = current + rate_list[moment] * diffused - advection_rate * advected
        adjoint = obs_weight * current
        for moment in reversed(range(STEPS)):
            adjoint_diffused, adjoint_slope = stencil_parts(rows_padded(adjoint))
            adjoint = (adjoint + rate_list[moment] * adjoint_diffused
                       + advection_rate * velocity[moment] * adjoint_slope
                       + advection_rate * history[moment] * state_slope[moment])
        return adjoint + prior_diag * probe

    product = lax.map(one_probe, directions)
    curvature = jnp.sum(directions * product, axis=(1, 2)) / (NROWS * COLS)
    return product, curvature
```

```python
import functools
import jax
import jax.numpy as jnp
from jax import lax
from jax.experimental import pallas as pl
from jax.experimental.pallas import tpu as pltpu
from jax.sharding import PartitionSpec as P

STEPS = 2
HALO = 4
TILE = 8


def pick_kernel(owners_ref, slot_ref, out_ref):
    out_ref[...] = jnp.broadcast_to(slot_ref[...][None], out_ref.shape)


def pick(owners, pieces, copies):
    slots, rows, cols = pieces.shape
    count = owners.shape[0]
    return pl.pallas_call(
        pick_kernel,
        out_shape=jax.ShapeDtypeStruct((copies, count, rows, cols), pieces.dtype),
        grid_spec=pltpu.PrefetchScalarGridSpec(
            num_scalar_prefetch=1,
            grid=(count,),
            in_specs=[pl.BlockSpec((1, rows, cols), lambda k, o: (o[k], 0, 0))],
            out_specs=pl.BlockSpec((copies, 1, rows, cols), lambda k, o: (0, k, 0, 0)),
        ),
    )(owners, pieces)


def upper(here, after):
    return jnp.concatenate([here[1:], after[:1]], axis=0)


def lower(before, here):
    return jnp.concatenate([before[-1:], here[:-1]], axis=0)


def stencil_kernel(
    edge_ref, steps_ref, rates_ref,
    dirs_hbm, ckpt_hbm, obs_hbm, prior_hbm,
    top_ref, bottom_ref, ctop_ref, cbottom_ref,
    product_hbm, curv_ref,
    state, ckpt, obs, prior, pa, qa, w1, pb, qb, out, acc, sems,
):
    dirs, rows, cols = dirs_hbm.shape
    tiles = rows // TILE
    main = pl.ds(TILE, rows)
    pieces = ckpt_hbm.shape[0]
    per = ckpt_hbm.shape[2]
    copies = [
        pltpu.make_async_copy(dirs_hbm, state.at[:, main], sems.at[0]),
        pltpu.make_async_copy(obs_hbm, obs.at[main], sems.at[1]),
        pltpu.make_async_copy(prior_hbm, prior, sems.at[2]),
    ]
    for piece in range(pieces):
        copies.append(
            pltpu.make_async_copy(
                ckpt_hbm.at[piece],
                ckpt.at[:, pl.ds(TILE + piece * per, per)],
                sems.at[3 + piece],
            )
        )
    for copy in copies:
        copy.start()
    for d in range(dirs):
        state[d, TILE - HALO:TILE] = top_ref[d]
        state[d, TILE + rows:TILE + rows + HALO] = bottom_ref[d]
    obs[TILE - HALO:TILE] = top_ref[dirs]
    obs[TILE + rows:TILE + rows + HALO] = bottom_ref[dirs]
    for k in range(2 * STEPS):
        ckpt[k, TILE - HALO:TILE] = ctop_ref[k]
        ckpt[k, TILE + rows:TILE + rows + HALO] = cbottom_ref[k]
    for copy in copies:
        copy.wait()
    r0 = rates_ref[steps_ref[0]]
    r1 = rates_ref[steps_ref[1]]
    s0 = 1.0 - 4.0 * r0
    s1 = 1.0 - 4.0 * r1
    has_top = edge_ref[0]
    has_bottom = edge_ref[1]
    column = lax.broadcasted_iota(jnp.int32, (TILE, cols), 1)
    first = column == 0
    last = column == cols - 1

    def right(x):
        return jnp.where(last, 0.0, pltpu.roll(x, cols - 1, 1))

    def left(x):
        return jnp.where(first, 0.0, pltpu.roll(x, 1, 1))

    def inside(t, x):
        keep = jnp.logical_or(
            jnp.logical_and(t > 0, t < tiles + 1),
            jnp.where(t == 0, has_top, has_bottom) > 0,
        )
        return jnp.where(keep, x, 0.0)

    def rows_of(t):
        return pl.ds(pl.multiple_of(t * TILE, TILE), TILE)

    def around(t):
        return (
            rows_of(jnp.maximum(t - 1, 0)),
            rows_of(t),
            rows_of(jnp.minimum(t + 1, tiles + 1)),
        )

    def first_pass(t, _):
        r = rows_of(t)
        lift = 0.125 * ckpt[0, r]
        for d in range(dirs):
            v = state[d, r]
            pa[d, r] = v * (r0 - lift)
            qa[d, r] = v * (r0 + lift)
        return 0

    def advance(t, scale, base, p, q, d):
        b, r, a = around(t)
        here_p = p[d, r]
        here_q = q[d, r]
        return (
            scale * base[d, r]
            + upper(here_p, p[d, a])
            + lower(q[d, b], here_q)
            + right(here_p)
            + left(here_q)
        )

    def second_pass(t, _):
        r = rows_of(t)
        lift = 0.125 * ckpt[1, r]
        for d in range(dirs):
            w = inside(t, advance(t, s0, state, pa, qa, d))
            w1[d, r] = w
            pb[d, r] = w * (r1 - lift)
            qb[d, r] = w * (r1 + lift)
        return 0

    def third_pass(t, _):
        r = rows_of(t)
        for d in range(dirs):
            w = inside(t, advance(t, s1, w1, pb, qb, d))
            pa[d, r] = obs[r] * w
        return 0

    def pull(t, rate, scale, vel, adj, hist, q, d):
        b, r, a = around(t)
        lift = 0.125 * ckpt[vel, r]
        slope = ckpt[adj, r]
        slope = 0.125 * (
            upper(slope, ckpt[adj, a]) - lower(ckpt[adj, b], slope) + right(slope) - left(slope)
        )
        here = q[d, r]
        return (
            scale * here
            + (rate + lift) * (upper(here, q[d, a]) + right(here))
            + (rate - lift) * (lower(q[d, b], here) + left(here))
            + hist[d, r] * slope
        )

    def fourth_pass(t, _):
        r = rows_of(t)
        for d in range(dirs):
            qa[d, r] = inside(t, pull(t, r1, s1, 1, 3, w1, pa, d))
        return 0

    def fifth_pass(t, _):
        r = rows_of(t)
        o = rows_of(t - 1)
        for d in range(dirs):
            v = state[d, r]
            value = pull(t, r0, s0, 0, 2, state, qa, d) + prior[o] * v
            out[d, o] = value
            acc[d] += v * value
        return 0

    acc[...] = jnp.zeros_like(acc)
    lax.fori_loop(0, tiles + 2, first_pass, 0)
    lax.fori_loop(0, tiles + 2, second_pass, 0)
    lax.fori_loop(0, tiles + 2, third_pass, 0)
    lax.fori_loop(0, tiles + 2, fourth_pass, 0)
    lax.fori_loop(1, tiles + 1, fifth_pass, 0)
    done = pltpu.make_async_copy(out, product_hbm, sems.at[0])
    done.start()
    for d in range(dirs):
        total = jnp.sum(acc[d], axis=(0, 1), keepdims=True)
        curv_ref[pl.ds(d, 1), :] = jnp.broadcast_to(total, (1, 128))
    done.wait()


def stencil(edge, steps, diffusion, dirs, ckpt, obs, prior, top, bottom, ctop, cbottom):
    count, rows, cols = dirs.shape
    ext = rows + 2 * TILE
    vmem = pl.BlockSpec(memory_space=pltpu.VMEM)
    smem = pl.BlockSpec(memory_space=pltpu.SMEM)
    anywhere = pl.BlockSpec(memory_space=pl.ANY)
    f32 = jnp.float32
    return pl.pallas_call(
        stencil_kernel,
        out_shape=(
            jax.ShapeDtypeStruct(dirs.shape, f32),
            jax.ShapeDtypeStruct((count, 128), f32),
        ),
        in_specs=[smem] * 3 + [anywhere] * 4 + [vmem] * 4,
        out_specs=(anywhere, vmem),
        scratch_shapes=[
            pltpu.VMEM((count, ext, cols), f32),
            pltpu.VMEM((2 * STEPS, ext, cols), f32),
            pltpu.VMEM((ext, cols), f32),
            pltpu.VMEM((rows, cols), f32),
        ]
        + [pltpu.VMEM((count, ext, cols), f32)] * 5
        + [
            pltpu.VMEM((count, rows, cols), f32),
            pltpu.VMEM((count, TILE, cols), f32),
            pltpu.SemaphoreType.DMA((3 + ckpt.shape[0],)),
        ],
        compiler_params=pltpu.CompilerParams(vmem_limit_bytes=60 * 1024 * 1024),
    )(edge, steps, diffusion, dirs, ckpt, obs, prior, top, bottom, ctop, cbottom)


def per_device(directions, pool, owners, window_steps, diffusion, obs_weight, prior_diag):
    peers = lax.axis_size("space")
    groups = lax.axis_size("dir")
    here = lax.axis_index("space")
    up = [(i, i + 1) for i in range(peers - 1)]
    down = [(j, i) for i, j in up]

    def halos(main):
        before = lax.ppermute(main[1], "space", up)
        after = lax.ppermute(main[0], "space", down)
        return before, after

    edge_first = jnp.concatenate([directions[:, :HALO], obs_weight[None, :HALO]], axis=0)
    edge_last = jnp.concatenate([directions[:, -HALO:], obs_weight[None, -HALO:]], axis=0)
    top, bottom = halos((edge_first, edge_last))

    pieces = lax.all_to_all(pool, "dir", 1, 0, tiled=True)
    chosen = pick(owners.reshape(-1), pieces, groups)
    ckpt = lax.all_to_all(chosen, "dir", 0, 0, tiled=True)
    ctop, cbottom = halos((ckpt[0, :, :HALO], ckpt[groups - 1, :, -HALO:]))

    edge = jnp.stack([here > 0, here < peers - 1]).astype(jnp.int32)
    product, partial_sums = stencil(
        edge, window_steps, diffusion, directions, ckpt, obs_weight, prior_diag,
        top, bottom, ctop, cbottom,
    )
    spread = jnp.broadcast_to(partial_sums[None], (peers,) + partial_sums.shape)
    gathered = lax.all_to_all(spread, "space", 0, 0, tiled=True)
    summed = jnp.sum(gathered, axis=0)[:, 0]
    cells = directions.shape[1] * peers * directions.shape[2]
    return (product, summed / cells)


def solution(mesh):
    return jax.shard_map(
        per_device,
        mesh=mesh,
        in_specs=(
            P("dir", "space", None),
            P("dir", "space", None),
            P(),
            P(),
            P(),
            P("space", None),
            P("space", None),
        ),
        out_specs=(P("dir", "space", None), P("dir")),
        check_vma=False,
    )
```

```python
import functools
import jax
import jax.numpy as jnp
from jax import lax
from jax.experimental import pallas as pl
from jax.experimental.pallas import tpu as pltpu
from jax.sharding import PartitionSpec as P

STEPS = 2
HALO = 4
TILE = 8
RING = 4
EDGES = 0
QUARTERS = 2
KEPT = 6
SOURCE = 7
PARITY = 11


def copy_kernel(meta_ref, from_ref, to_ref):
    to_ref[...] = from_ref[...].reshape(to_ref.shape)


def gather_blocks(meta, source, grid, in_block, in_map, out_shape, out_block, out_map):
    return pl.pallas_call(
        copy_kernel,
        out_shape=jax.ShapeDtypeStruct(out_shape, source.dtype),
        grid_spec=pltpu.PrefetchScalarGridSpec(
            num_scalar_prefetch=1,
            grid=grid,
            in_specs=[pl.BlockSpec(in_block, in_map)],
            out_specs=pl.BlockSpec(out_block, out_map),
        ),
    )(meta, source)


def upper(here, after):
    return jnp.concatenate([here[1:], after[:1]], axis=0)


def lower(before, here):
    return jnp.concatenate([before[-1:], here[:-1]], axis=0)


def stencil_kernel(
    meta_ref, steps_ref, rates_ref,
    dirs_hbm, own_hbm, before_hbm, after_hbm, across_hbm, obs_hbm, prior_hbm,
    top_ref, bottom_ref, ctop_ref, cbottom_ref,
    product_hbm, curv_ref,
    state, ckpt, obs, prior, pa, qa, w1, pb, qb, out, acc, sems,
):
    dirs, rows, cols = dirs_hbm.shape
    tiles = rows // TILE
    main = pl.ds(TILE, rows)
    pieces = (own_hbm, before_hbm, after_hbm, across_hbm)
    per = own_hbm.shape[1]
    copies = [
        pltpu.make_async_copy(dirs_hbm, state.at[:, main], sems.at[0]),
        pltpu.make_async_copy(obs_hbm, obs.at[main], sems.at[1]),
        pltpu.make_async_copy(prior_hbm, prior, sems.at[2]),
    ]
    for i, piece in enumerate(pieces):
        place = pl.multiple_of(TILE + per * meta_ref[QUARTERS + i], TILE)
        copies.append(
            pltpu.make_async_copy(piece, ckpt.at[:, pl.ds(place, per)], sems.at[3 + i])
        )
    for copy in copies:
        copy.start()
    for d in range(dirs):
        state[d, TILE - HALO:TILE] = top_ref[d]
        state[d, TILE + rows:TILE + rows + HALO] = bottom_ref[d]
    obs[TILE - HALO:TILE] = top_ref[dirs]
    obs[TILE + rows:TILE + rows + HALO] = bottom_ref[dirs]
    for k in range(2 * STEPS):
        ckpt[k, TILE - HALO:TILE] = ctop_ref[k]
        ckpt[k, TILE + rows:TILE + rows + HALO] = cbottom_ref[k]
    for copy in copies:
        copy.wait()
    r0 = rates_ref[steps_ref[0]]
    r1 = rates_ref[steps_ref[1]]
    s0 = 1.0 - 4.0 * r0
    s1 = 1.0 - 4.0 * r1
    has_top = meta_ref[EDGES]
    has_bottom = meta_ref[EDGES + 1]
    column = lax.broadcasted_iota(jnp.int32, (TILE, cols), 1)
    first = column == 0
    last = column == cols - 1

    def right(x):
        return jnp.where(last, 0.0, pltpu.roll(x, cols - 1, 1))

    def left(x):
        return jnp.where(first, 0.0, pltpu.roll(x, 1, 1))

    def inside(t, x):
        keep = jnp.logical_or(
            jnp.logical_and(t > 0, t < tiles + 1),
            jnp.where(t == 0, has_top, has_bottom) > 0,
        )
        return jnp.where(keep, x, 0.0)

    def rows_of(t):
        return pl.ds(pl.multiple_of(t * TILE, TILE), TILE)

    def around(t):
        return (
            rows_of(jnp.maximum(t - 1, 0)),
            rows_of(t),
            rows_of(jnp.minimum(t + 1, tiles + 1)),
        )

    def first_pass(t, _):
        r = rows_of(t)
        lift = 0.125 * ckpt[0, r]
        for d in range(dirs):
            v = state[d, r]
            pa[d, r] = v * (r0 - lift)
            qa[d, r] = v * (r0 + lift)
        return 0

    def advance(t, scale, base, p, q, d):
        b, r, a = around(t)
        here_p = p[d, r]
        here_q = q[d, r]
        return (
            scale * base[d, r]
            + upper(here_p, p[d, a])
            + lower(q[d, b], here_q)
            + right(here_p)
            + left(here_q)
        )

    def second_pass(t, _):
        r = rows_of(t)
        lift = 0.125 * ckpt[1, r]
        for d in range(dirs):
            w = inside(t, advance(t, s0, state, pa, qa, d))
            w1[d, r] = w
            pb[d, r] = w * (r1 - lift)
            qb[d, r] = w * (r1 + lift)
        return 0

    def third_pass(t, _):
        r = rows_of(t)
        for d in range(dirs):
            w = inside(t, advance(t, s1, w1, pb, qb, d))
            pa[d, r] = obs[r] * w
        return 0

    def pull(t, rate, scale, vel, adj, hist, q, d):
        b, r, a = around(t)
        lift = 0.125 * ckpt[vel, r]
        slope = ckpt[adj, r]
        slope = 0.125 * (
            upper(slope, ckpt[adj, a]) - lower(ckpt[adj, b], slope) + right(slope) - left(slope)
        )
        here = q[d, r]
        return (
            scale * here
            + (rate + lift) * (upper(here, q[d, a]) + right(here))
            + (rate - lift) * (lower(q[d, b], here) + left(here))
            + hist[d, r] * slope
        )

    def fourth_pass(t, _):
        r = rows_of(t)
        for d in range(dirs):
            qa[d, r] = inside(t, pull(t, r1, s1, 1, 3, w1, pa, d))
        return 0

    def fifth_pass(t, _):
        r = rows_of(t)
        o = rows_of(t - 1)
        for d in range(dirs):
            v = state[d, r]
            value = pull(t, r0, s0, 0, 2, state, qa, d) + prior[o] * v
            out[d, o] = value
            acc[d] += v * value
        return 0

    acc[...] = jnp.zeros_like(acc)
    lax.fori_loop(0, tiles + 2, first_pass, 0)
    lax.fori_loop(0, tiles + 2, second_pass, 0)
    lax.fori_loop(0, tiles + 2, third_pass, 0)
    lax.fori_loop(0, tiles + 2, fourth_pass, 0)
    lax.fori_loop(1, tiles + 1, fifth_pass, 0)
    done = pltpu.make_async_copy(out, product_hbm, sems.at[0])
    done.start()
    for d in range(dirs):
        total = jnp.sum(acc[d], axis=(0, 1), keepdims=True)
        curv_ref[pl.ds(d, 1), :] = jnp.broadcast_to(total, (1, 128))
    done.wait()


def stencil(meta, steps, diffusion, dirs, pieces, obs, prior, top, bottom, ctop, cbottom):
    count, rows, cols = dirs.shape
    ext = rows + 2 * TILE
    vmem = pl.BlockSpec(memory_space=pltpu.VMEM)
    smem = pl.BlockSpec(memory_space=pltpu.SMEM)
    anywhere = pl.BlockSpec(memory_space=pl.ANY)
    f32 = jnp.float32
    return pl.pallas_call(
        stencil_kernel,
        out_shape=(
            jax.ShapeDtypeStruct(dirs.shape, f32),
            jax.ShapeDtypeStruct((count, 128), f32),
        ),
        in_specs=[smem] * 3 + [anywhere] * 7 + [vmem] * 4,
        out_specs=(anywhere, vmem),
        scratch_shapes=[
            pltpu.VMEM((count, ext, cols), f32),
            pltpu.VMEM((2 * STEPS, ext, cols), f32),
            pltpu.VMEM((ext, cols), f32),
            pltpu.VMEM((rows, cols), f32),
        ]
        + [pltpu.VMEM((count, ext, cols), f32)] * 5
        + [
            pltpu.VMEM((count, rows, cols), f32),
            pltpu.VMEM((count, TILE, cols), f32),
            pltpu.SemaphoreType.DMA((3 + len(pieces),)),
        ],
        compiler_params=pltpu.CompilerParams(vmem_limit_bytes=36 * 1024 * 1024),
    )(meta, steps, diffusion, dirs, *pieces, obs, prior, top, bottom, ctop, cbottom)


def per_device(directions, pool, owners, window_steps, diffusion, obs_weight, prior_diag):
    peers = lax.axis_size("space")
    groups = lax.axis_size("dir")
    here = lax.axis_index("space")
    group = lax.axis_index("dir")
    slots, rows, cols = pool.shape
    rings = groups // RING
    quarter = rows // RING
    up = [(i, i + 1) for i in range(peers - 1)]
    down = [(j, i) for i, j in up]
    forward = [(r * RING + y, r * RING + (y + 1) % RING) for r in range(rings) for y in range(RING)]
    backward = [(j, i) for i, j in forward]
    swap = [(i, (i + RING) % groups) for i in range(groups)]

    wanted = owners.reshape(-1)
    holder = wanted // slots
    parity = wanted % slots
    mine = (group % RING) + 2 * (group // RING)
    keeps_first = jnp.any(wanted == group * slots)
    shared = jnp.sum((holder[:, None] == holder[None, :]).astype(jnp.int32)) > wanted.shape[0]
    meta = jnp.concatenate(
        [
            jnp.stack(
                [
                    here > 0,
                    here < peers - 1,
                    mine % RING,
                    (mine + 3) % RING,
                    (mine + 1) % RING,
                    (mine + 2) % RING,
                    1 - keeps_first.astype(jnp.int32),
                ]
            ).astype(jnp.int32),
            holder,
            parity,
        ]
    ).astype(jnp.int32)

    def part(i):
        return (i + 2 * (i // RING)) % RING

    def scatter(width):
        if width == 1:
            in_map = lambda i, m: (m[KEPT], part(i), 0)
            pick_map = lambda k, m: (m[SOURCE + k], 0, 0, 0)
        else:
            in_map = lambda i, m: (0, part(i), 0)
            pick_map = lambda k, m: (m[SOURCE + k], m[PARITY + k], 0, 0)

        def run(meta, pool, first, last):
            blocks = gather_blocks(
                meta, pool, (groups,), (width, quarter, cols), in_map,
                (groups, width, quarter, cols), (1, width, quarter, cols),
                lambda i, m: (i, 0, 0, 0),
            )
            blocks = lax.all_to_all(blocks, "dir", 0, 0, tiled=True)
            before = lax.ppermute(last, "space", up)
            after = lax.ppermute(first, "space", down)
            own = gather_blocks(
                meta, blocks, (2 * STEPS,), (1, 1, quarter, cols), pick_map,
                (2 * STEPS, quarter, cols), (1, quarter, cols),
                lambda k, m: (k, 0, 0),
            )
            return own, before, after

        return run

    edge_first = jnp.concatenate([directions[:, :HALO], obs_weight[None, :HALO]], axis=0)
    edge_last = jnp.concatenate([directions[:, -HALO:], obs_weight[None, -HALO:]], axis=0)
    own, top, bottom = lax.cond(
        shared, scatter(slots), scatter(1), meta, pool, edge_first, edge_last
    )
    across = lax.ppermute(own, "dir", swap)
    before = lax.ppermute(own, "dir", forward)
    after = lax.ppermute(own, "dir", backward)

    def holding(q, take):
        return jnp.where(
            meta[QUARTERS] == q,
            take(own),
            jnp.where(
                meta[QUARTERS + 1] == q,
                take(before),
                jnp.where(meta[QUARTERS + 2] == q, take(after), take(across)),
            ),
        )

    ctop = lax.ppermute(holding(RING - 1, lambda x: x[:, -HALO:]), "space", up)
    cbottom = lax.ppermute(holding(0, lambda x: x[:, :HALO]), "space", down)
    product, partial_sums = stencil(
        meta, window_steps, diffusion, directions, (own, before, after, across),
        obs_weight, prior_diag, top, bottom, ctop, cbottom,
    )
    spread = jnp.broadcast_to(partial_sums[None], (peers,) + partial_sums.shape)
    gathered = lax.all_to_all(spread, "space", 0, 0, tiled=True)
    summed = jnp.sum(gathered, axis=0)[:, 0]
    cells = directions.shape[1] * peers * directions.shape[2]
    return (product, summed / cells)


def solution(mesh):
    return jax.shard_map(
        per_device,
        mesh=mesh,
        in_specs=(
            P("dir", "space", None),
            P("dir", "space", None),
            P(),
            P(),
            P(),
            P("space", None),
            P("space", None),
        ),
        out_specs=(P("dir", "space", None), P("dir")),
        check_vma=False,
    )
```

```python
import functools
import jax
import jax.numpy as jnp
from jax import lax
from jax.experimental import pallas as pl
from jax.experimental.pallas import tpu as pltpu
from jax.sharding import PartitionSpec as P

STEPS = 2
HALO = 4
TILE = 8
LANES = 128
SUMS = 4
RING = 4
EDGES = 0
QUARTERS = 2
KEPT = 6
SOURCE = 7
PARITY = 11
SHARED = 15


def meta_kernel(slots, owners_ref, meta_ref):
    group = lax.axis_index("dir")
    here = lax.axis_index("space")
    peers = lax.axis_size("space")
    mine = lax.rem(group, RING) + 2 * lax.div(group, RING)
    meta_ref[EDGES] = (here > 0).astype(jnp.int32)
    meta_ref[EDGES + 1] = (here < peers - 1).astype(jnp.int32)
    for i, step in enumerate((0, 3, 1, 2)):
        meta_ref[QUARTERS + i] = lax.rem(mine + step, RING)
    wanted = [owners_ref[k // STEPS, k % STEPS] for k in range(2 * STEPS)]
    holders = [lax.div(w, slots) for w in wanted]
    kept = jnp.int32(1)
    shared = jnp.int32(0)
    for k, w in enumerate(wanted):
        kept = jnp.where(w == group * slots, 0, kept)
        for other in holders[:k]:
            shared = jnp.where(other == holders[k], 1, shared)
        meta_ref[SOURCE + k] = holders[k]
        meta_ref[PARITY + k] = lax.rem(w, slots)
    meta_ref[KEPT] = kept
    meta_ref[SHARED] = shared


def part(i):
    return (i + 2 * (i // RING)) % RING


def spread_kernel(meta_ref, pool_ref, out_ref, held, in_sems, out_sems):
    groups, width, quarter, _ = out_ref.shape
    begin = meta_ref[KEPT] if width == 1 else 0
    loads = []
    for q in range(RING):
        rows = pl.ds(q * quarter, quarter)
        copy = pltpu.make_async_copy(
            pool_ref.at[pl.ds(begin, width), rows], held.at[:, rows], in_sems.at[q]
        )
        copy.start()
        loads.append(copy)
    stores = []
    for q in range(RING):
        loads[q].wait()
        for i in range(groups):
            if part(i) == q:
                copy = pltpu.make_async_copy(
                    held.at[:, pl.ds(q * quarter, quarter)], out_ref.at[i], out_sems.at[i]
                )
                copy.start()
                stores.append(copy)
    for copy in stores:
        copy.wait()


def pick_kernel(meta_ref, blocks_ref, own_ref, sems):
    width = blocks_ref.shape[1]
    copies = []
    for k in range(own_ref.shape[0]):
        slot = meta_ref[PARITY + k] if width > 1 else 0
        copy = pltpu.make_async_copy(
            blocks_ref.at[meta_ref[SOURCE + k], slot], own_ref.at[k], sems.at[k]
        )
        copy.start()
        copies.append(copy)
    for copy in copies:
        copy.wait()


def stencil_kernel(
    meta_ref, steps_ref, rates_ref,
    dirs_hbm, own_hbm, before_hbm, after_hbm, across_hbm, obs_hbm, prior_hbm,
    top_ref, bottom_ref, ctop_ref, cbottom_ref,
    product_hbm, curv_ref,
    state, ckpt, obs, prior, pa, qa, w1, pb, qb, out, sems,
):
    dirs, rows, cols = dirs_hbm.shape
    tiles = rows // TILE
    blocks = cols // LANES
    main = pl.ds(TILE, rows)
    middle = pl.ds(LANES, cols)
    pieces = (own_hbm, before_hbm, after_hbm, across_hbm)
    per = own_hbm.shape[1]
    first_copies = [pltpu.make_async_copy(dirs_hbm, state.at[:, main], sems.at[0])]
    for i, piece in enumerate(pieces):
        place = pl.multiple_of(TILE + per * meta_ref[QUARTERS + i], TILE)
        first_copies.append(
            pltpu.make_async_copy(
                piece, ckpt.at[:, pl.ds(place, per), middle], sems.at[3 + i]
            )
        )
    obs_copy = pltpu.make_async_copy(obs_hbm, obs.at[main], sems.at[1])
    prior_copy = pltpu.make_async_copy(prior_hbm, prior, sems.at[2])
    for copy in first_copies + [obs_copy, prior_copy]:
        copy.start()
    above = pl.ds(TILE - HALO, HALO)
    below = pl.ds(TILE + rows, HALO)
    for d in range(dirs):
        state[d, above] = top_ref[d]
        state[d, below] = bottom_ref[d]
    obs[above] = top_ref[dirs]
    obs[below] = bottom_ref[dirs]
    for k in range(2 * STEPS):
        ckpt[k, above, middle] = ctop_ref[k]
        ckpt[k, below, middle] = cbottom_ref[k]
    ext = rows + 2 * TILE
    blank = jnp.zeros((ext, LANES), jnp.float32)
    for ref in (pa, qa, pb, qb):
        for d in range(dirs):
            ref[d, :, pl.ds(0, LANES)] = blank
            ref[d, :, pl.ds(LANES + cols, LANES)] = blank
    for k in range(STEPS, 2 * STEPS):
        ckpt[k, :, pl.ds(0, LANES)] = blank
        ckpt[k, :, pl.ds(LANES + cols, LANES)] = blank
    for copy in first_copies:
        copy.wait()
    r0 = rates_ref[steps_ref[0]]
    r1 = rates_ref[steps_ref[1]]
    s0 = 1.0 - 4.0 * r0
    s1 = 1.0 - 4.0 * r1
    row = lax.broadcasted_iota(jnp.int32, (TILE, LANES), 0)
    lane = lax.broadcasted_iota(jnp.int32, (TILE, LANES), 1)
    row_first = row == 0
    row_last = row == TILE - 1
    lane_first = lane == 0
    lane_last = lane == LANES - 1

    def upper(here, after):
        return pltpu.roll(jnp.where(row_first, after, here), TILE - 1, 0)

    def lower(before, here):
        return pltpu.roll(jnp.where(row_last, before, here), 1, 0)

    def right(here, after):
        return pltpu.roll(jnp.where(lane_first, after, here), LANES - 1, 1)

    def left(before, here):
        return pltpu.roll(jnp.where(lane_last, before, here), 1, 1)

    def rows_of(t):
        return pl.ds(pl.multiple_of(t * TILE, TILE), TILE)

    def around(t):
        return (
            rows_of(jnp.maximum(t - 1, 0)),
            rows_of(t),
            rows_of(jnp.minimum(t + 1, tiles + 1)),
        )

    def wide(c):
        return pl.ds((c + 1) * LANES, LANES)

    def thin(c):
        return pl.ds(c * LANES, LANES)

    def row_reader(ref, index, r):
        seen = {}

        def read(c):
            if c not in seen:
                seen[c] = ref[index, r, wide(c)]
            return seen[c]

        return read

    def first_pass(t, _):
        r = rows_of(t)
        for c in range(blocks):
            lift = 0.125 * ckpt[0, r, wide(c)]
            down = r0 - lift
            rise = r0 + lift
            for d in range(dirs):
                v = state[d, r, thin(c)]
                pa[d, r, wide(c)] = v * down
                qa[d, r, wide(c)] = v * rise
        return 0

    def advance(c, scale, base, ps, qs, d, p, q, b, a):
        here_p = ps[d](c)
        here_q = qs[d](c)
        return (
            scale * base
            + (upper(here_p, p[d, a, wide(c)]) + lower(q[d, b, wide(c)], here_q))
            + (right(here_p, ps[d](c + 1)) + left(qs[d](c - 1), here_q))
        )

    def second_pass(t, _):
        b, r, a = around(t)
        ps = [row_reader(pa, d, r) for d in range(dirs)]
        qs = [row_reader(qa, d, r) for d in range(dirs)]
        for c in range(blocks):
            lift = 0.125 * ckpt[1, r, wide(c)]
            down = r1 - lift
            rise = r1 + lift
            for d in range(dirs):
                w = advance(c, s0, state[d, r, thin(c)], ps, qs, d, pa, qa, b, a)
                w1[d, r, thin(c)] = w
                pb[d, r, wide(c)] = w * down
                qb[d, r, wide(c)] = w * rise
        return 0

    def third_pass(t, _):
        b, r, a = around(t)
        ps = [row_reader(pb, d, r) for d in range(dirs)]
        qs = [row_reader(qb, d, r) for d in range(dirs)]
        for c in range(blocks):
            weight = obs[r, thin(c)]
            for d in range(dirs):
                w = advance(c, s1, w1[d, r, thin(c)], ps, qs, d, pb, qb, b, a)
                pa[d, r, wide(c)] = weight * w
        return 0

    def pull(t, rate, scale, vel, adj, hist, q, emit):
        b, r, a = around(t)
        slopes = row_reader(ckpt, adj, r)
        readers = [row_reader(q, d, r) for d in range(dirs)]
        for c in range(blocks):
            lift = 0.125 * ckpt[vel, r, wide(c)]
            rise = rate + lift
            down = rate - lift
            here = slopes(c)
            slope = 0.125 * (
                (upper(here, ckpt[adj, a, wide(c)]) + right(here, slopes(c + 1)))
                - (lower(ckpt[adj, b, wide(c)], here) + left(slopes(c - 1), here))
            )
            for d in range(dirs):
                here = readers[d](c)
                plus = upper(here, q[d, a, wide(c)]) + right(here, readers[d](c + 1))
                minus = lower(q[d, b, wide(c)], here) + left(readers[d](c - 1), here)
                past = hist[d, r, thin(c)]
                emit(c, d, past, (scale * here + past * slope) + (rise * plus + down * minus))

    def fourth_pass(t, _):
        r = rows_of(t)

        def emit(c, d, past, value):
            qa[d, r, wide(c)] = value

        pull(t, r1, s1, 1, 3, w1, pa, emit)
        return 0

    half = tiles // 2

    def out_copy(part):
        span = pl.ds(part * half * TILE, half * TILE)
        return pltpu.make_async_copy(
            out.at[:, span], product_hbm.at[:, span], sems.at[part]
        )

    def fifth_pass(t, sums):
        sums = list(sums)
        o = rows_of(t - 1)

        def emit(c, d, past, value):
            value = value + prior[o, thin(c)] * past
            out[d, o, thin(c)] = value
            lot = d * SUMS + c % SUMS
            sums[lot] = sums[lot] + past * value

        pull(t, r0, s0, 0, 2, state, qa, emit)

        @pl.when(t == half)
        def _():
            out_copy(0).start()

        return tuple(sums)

    def close_edges(refs, at):
        for flag, t in ((0, 0), (1, tiles + 1)):

            @pl.when(meta_ref[EDGES + flag] == 0)
            def _():
                for ref in refs:
                    for d in range(dirs):
                        ref[d, pl.ds(t * TILE, TILE), at] = jnp.zeros((TILE, cols), jnp.float32)

    lax.fori_loop(0, tiles + 2, first_pass, 0)
    lax.fori_loop(0, tiles + 2, second_pass, 0)
    close_edges((pb, qb), middle)
    close_edges((w1,), pl.ds(0, cols))
    obs_copy.wait()
    lax.fori_loop(0, tiles + 2, third_pass, 0)
    close_edges((pa,), middle)
    lax.fori_loop(0, tiles + 2, fourth_pass, 0)
    close_edges((qa,), middle)
    prior_copy.wait()
    zero = jnp.zeros((TILE, LANES), jnp.float32)
    sums = lax.fori_loop(1, tiles + 1, fifth_pass, (zero,) * (SUMS * dirs))
    out_copy(1).start()
    for d in range(dirs):
        total = sums[d * SUMS]
        for lot in range(1, SUMS):
            total = total + sums[d * SUMS + lot]
        total = jnp.sum(total, axis=(0, 1), keepdims=True)
        curv_ref[pl.ds(d, 1), :] = jnp.broadcast_to(total, (1, LANES))
    out_copy(0).wait()
    out_copy(1).wait()


def stencil(meta, steps, diffusion, dirs, pieces, obs, prior, top, bottom, ctop, cbottom):
    count, rows, cols = dirs.shape
    ext = rows + 2 * TILE
    wide = cols + 2 * LANES
    vmem = pl.BlockSpec(memory_space=pltpu.VMEM)
    smem = pl.BlockSpec(memory_space=pltpu.SMEM)
    anywhere = pl.BlockSpec(memory_space=pl.ANY)
    f32 = jnp.float32
    return pl.pallas_call(
        stencil_kernel,
        out_shape=(
            jax.ShapeDtypeStruct(dirs.shape, f32),
            jax.ShapeDtypeStruct((count, 128), f32),
        ),
        in_specs=[smem] * 3 + [anywhere] * 7 + [vmem] * 4,
        out_specs=(anywhere, vmem),
        scratch_shapes=[
            pltpu.VMEM((count, ext, cols), f32),
            pltpu.VMEM((2 * STEPS, ext, wide), f32),
            pltpu.VMEM((ext, cols), f32),
            pltpu.VMEM((rows, cols), f32),
            pltpu.VMEM((count, ext, wide), f32),
            pltpu.VMEM((count, ext, wide), f32),
            pltpu.VMEM((count, ext, cols), f32),
            pltpu.VMEM((count, ext, wide), f32),
            pltpu.VMEM((count, ext, wide), f32),
            pltpu.VMEM((count, rows, cols), f32),
            pltpu.SemaphoreType.DMA((3 + len(pieces),)),
        ],
        compiler_params=pltpu.CompilerParams(vmem_limit_bytes=34 * 1024 * 1024),
    )(meta, steps, diffusion, dirs, *pieces, obs, prior, top, bottom, ctop, cbottom)


def per_device(directions, pool, owners, window_steps, diffusion, obs_weight, prior_diag):
    peers = lax.axis_size("space")
    groups = lax.axis_size("dir")
    slots, rows, cols = pool.shape
    rings = groups // RING
    quarter = rows // RING
    up = [(i, i + 1) for i in range(peers - 1)]
    down = [(j, i) for i, j in up]
    forward = [(r * RING + y, r * RING + (y + 1) % RING) for r in range(rings) for y in range(RING)]
    backward = [(j, i) for i, j in forward]
    swap = [(i, (i + RING) % groups) for i in range(groups)]

    smem = pl.BlockSpec(memory_space=pltpu.SMEM)
    anywhere = pl.BlockSpec(memory_space=pl.ANY)
    meta = pl.pallas_call(
        functools.partial(meta_kernel, slots),
        out_shape=jax.ShapeDtypeStruct((SHARED + 1,), jnp.int32),
        in_specs=[smem],
        out_specs=smem,
    )(owners)

    def scatter(width):
        def run(meta, pool, directions, obs_weight):
            blocks = pl.pallas_call(
                spread_kernel,
                out_shape=jax.ShapeDtypeStruct((groups, width, quarter, cols), pool.dtype),
                in_specs=[smem, anywhere],
                out_specs=anywhere,
                scratch_shapes=[
                    pltpu.VMEM((width, rows, cols), pool.dtype),
                    pltpu.SemaphoreType.DMA((RING,)),
                    pltpu.SemaphoreType.DMA((groups,)),
                ],
            )(meta, pool)
            blocks = lax.all_to_all(blocks, "dir", 0, 0, tiled=True)
            first = jnp.concatenate([directions[:, :HALO], obs_weight[None, :HALO]], axis=0)
            last = jnp.concatenate([directions[:, -HALO:], obs_weight[None, -HALO:]], axis=0)
            before = lax.ppermute(last, "space", up)
            after = lax.ppermute(first, "space", down)
            own = pl.pallas_call(
                pick_kernel,
                out_shape=jax.ShapeDtypeStruct((2 * STEPS, quarter, cols), pool.dtype),
                in_specs=[smem, anywhere],
                out_specs=pl.BlockSpec(memory_space=pltpu.VMEM),
                scratch_shapes=[pltpu.SemaphoreType.DMA((2 * STEPS,))],
            )(meta, blocks)
            return own, before, after

        return run

    own, top, bottom = lax.cond(
        meta[SHARED] > 0, scatter(slots), scatter(1), meta, pool, directions, obs_weight
    )
    across = lax.ppermute(own, "dir", swap)
    before = lax.ppermute(own, "dir", forward)
    after = lax.ppermute(own, "dir", backward)

    def holding(q, take):
        return jnp.where(
            meta[QUARTERS] == q,
            take(own),
            jnp.where(
                meta[QUARTERS + 1] == q,
                take(before),
                jnp.where(meta[QUARTERS + 2] == q, take(after), take(across)),
            ),
        )

    ctop = lax.ppermute(holding(RING - 1, lambda x: x[:, -HALO:]), "space", up)
    cbottom = lax.ppermute(holding(0, lambda x: x[:, :HALO]), "space", down)
    product, partial_sums = stencil(
        meta, window_steps, diffusion, directions, (own, before, after, across),
        obs_weight, prior_diag, top, bottom, ctop, cbottom,
    )
    spread = jnp.broadcast_to(partial_sums[None], (peers,) + partial_sums.shape)
    gathered = lax.all_to_all(spread, "space", 0, 0, tiled=True)
    summed = jnp.sum(gathered, axis=0)[:, 0]
    cells = directions.shape[1] * peers * directions.shape[2]
    return (product, summed / cells)


def solution(mesh):
    return jax.shard_map(
        per_device,
        mesh=mesh,
        in_specs=(
            P("dir", "space", None),
            P("dir", "space", None),
            P(),
            P(),
            P(),
            P("space", None),
            P("space", None),
        ),
        out_specs=(P("dir", "space", None), P("dir")),
        check_vma=False,
    )
```

```python
import functools
import jax
import jax.numpy as jnp
from jax import lax
from jax.experimental import pallas as pl
from jax.experimental.pallas import tpu as pltpu
from jax.sharding import PartitionSpec as P

STEPS = 2
HALO = 4
TILE = 8
LANES = 128
SUMS = 4
RING = 4
EDGES = 0
QUARTERS = 2
KEPT = 6
SOURCE = 7
PARITY = 11
SHARED = 15
OFFSETS = ((1, 2), (1, 1), (1, 3), (0, 2), (1, 0), (0, 1), (0, 3))


def meta_kernel(slots, owners_ref, meta_ref):
    group = lax.axis_index("dir")
    here = lax.axis_index("space")
    peers = lax.axis_size("space")
    rings = lax.axis_size("dir") // RING
    column = lax.div(group, RING)
    place = lax.rem(group, RING)
    mine = place + 2 * column
    meta_ref[EDGES] = (here > 0).astype(jnp.int32)
    meta_ref[EDGES + 1] = (here < peers - 1).astype(jnp.int32)
    for i, step in enumerate((0, 3, 1, 2)):
        meta_ref[QUARTERS + i] = lax.rem(mine + step, RING)
    wanted = [owners_ref[k // STEPS, k % STEPS] for k in range(2 * STEPS)]
    holders = [lax.div(w, slots) for w in wanted]
    kept = jnp.int32(1)
    shared = jnp.int32(0)
    for k, w in enumerate(wanted):
        kept = jnp.where(w == group * slots, 0, kept)
        for other in holders[:k]:
            shared = jnp.where(other == holders[k], 1, shared)
        across = lax.rem(column + rings - lax.div(holders[k], RING), rings)
        along = lax.rem(place + RING - lax.rem(holders[k], RING), RING)
        meta_ref[SOURCE + k] = across * RING + along
        meta_ref[PARITY + k] = lax.rem(w, slots)
    meta_ref[KEPT] = kept
    meta_ref[SHARED] = shared


def quarters_kernel(meta_ref, pool_ref, *refs):
    outs, sems = refs[:RING], refs[RING]
    width, quarter, _ = outs[0].shape
    begin = meta_ref[KEPT] if width == 1 else 0
    copies = []
    for q, out_ref in enumerate(outs):
        place = lax.rem(meta_ref[QUARTERS] + q, RING) * quarter
        rows = pl.ds(pl.multiple_of(place, TILE), quarter)
        copy = pltpu.make_async_copy(
            pool_ref.at[pl.ds(begin, width), rows], out_ref, sems.at[q]
        )
        copy.start()
        copies.append(copy)
    for copy in copies:
        copy.wait()


def pick_kernel(meta_ref, *refs):
    parts, own_ref, sems = refs[:-2], refs[-2], refs[-1]
    width = parts[0].shape[0]
    for k in range(own_ref.shape[0]):
        slot = meta_ref[PARITY + k] if width > 1 else 0
        for j, part_ref in enumerate(parts):

            @pl.when(meta_ref[SOURCE + k] == j)
            def _():
                pltpu.make_async_copy(part_ref.at[slot], own_ref.at[k], sems.at[k]).start()

    for k in range(own_ref.shape[0]):
        pltpu.make_async_copy(parts[0].at[0], own_ref.at[k], sems.at[k]).wait()


def stencil_kernel(
    meta_ref, steps_ref, rates_ref,
    dirs_hbm, own_hbm, before_hbm, after_hbm, across_hbm, obs_hbm, prior_hbm,
    top_ref, bottom_ref, ctop_ref, cbottom_ref,
    product_hbm, curv_ref,
    state, ckpt, obs, prior, pa, qa, w1, pb, qb, out, sems,
):
    dirs, rows, cols = dirs_hbm.shape
    tiles = rows // TILE
    blocks = cols // LANES
    main = pl.ds(TILE, rows)
    middle = pl.ds(LANES, cols)
    pieces = (own_hbm, before_hbm, after_hbm, across_hbm)
    per = own_hbm.shape[1]
    first_copies = [pltpu.make_async_copy(dirs_hbm, state.at[:, main], sems.at[0])]
    for i, piece in enumerate(pieces):
        place = pl.multiple_of(TILE + per * meta_ref[QUARTERS + i], TILE)
        first_copies.append(
            pltpu.make_async_copy(
                piece, ckpt.at[:, pl.ds(place, per), middle], sems.at[3 + i]
            )
        )
    obs_copy = pltpu.make_async_copy(obs_hbm, obs.at[main], sems.at[1])
    prior_copy = pltpu.make_async_copy(prior_hbm, prior, sems.at[2])
    for copy in first_copies + [obs_copy, prior_copy]:
        copy.start()
    above = pl.ds(TILE - HALO, HALO)
    below = pl.ds(TILE + rows, HALO)
    for d in range(dirs):
        state[d, above] = top_ref[d]
        state[d, below] = bottom_ref[d]
    obs[above] = top_ref[dirs]
    obs[below] = bottom_ref[dirs]
    for k in range(2 * STEPS):
        ckpt[k, above, middle] = ctop_ref[k]
        ckpt[k, below, middle] = cbottom_ref[k]
    ext = rows + 2 * TILE
    blank = jnp.zeros((ext, LANES), jnp.float32)
    for ref in (pa, qa, pb, qb):
        for d in range(dirs):
            ref[d, :, pl.ds(0, LANES)] = blank
            ref[d, :, pl.ds(LANES + cols, LANES)] = blank
    for k in range(STEPS, 2 * STEPS):
        ckpt[k, :, pl.ds(0, LANES)] = blank
        ckpt[k, :, pl.ds(LANES + cols, LANES)] = blank
    for copy in first_copies:
        copy.wait()
    r0 = rates_ref[steps_ref[0]]
    r1 = rates_ref[steps_ref[1]]
    s0 = 1.0 - 4.0 * r0
    s1 = 1.0 - 4.0 * r1
    row = lax.broadcasted_iota(jnp.int32, (TILE, LANES), 0)
    lane = lax.broadcasted_iota(jnp.int32, (TILE, LANES), 1)
    row_first = row == 0
    row_last = row == TILE - 1
    lane_first = lane == 0
    lane_last = lane == LANES - 1

    def upper(here, after):
        return pltpu.roll(jnp.where(row_first, after, here), TILE - 1, 0)

    def lower(before, here):
        return pltpu.roll(jnp.where(row_last, before, here), 1, 0)

    def right(here, after):
        return pltpu.roll(jnp.where(lane_first, after, here), LANES - 1, 1)

    def left(before, here):
        return pltpu.roll(jnp.where(lane_last, before, here), 1, 1)

    def rows_of(t):
        return pl.ds(pl.multiple_of(t * TILE, TILE), TILE)

    def around(t):
        return (
            rows_of(jnp.maximum(t - 1, 0)),
            rows_of(t),
            rows_of(jnp.minimum(t + 1, tiles + 1)),
        )

    def wide(c):
        return pl.ds((c + 1) * LANES, LANES)

    def thin(c):
        return pl.ds(c * LANES, LANES)

    def row_reader(ref, index, r):
        seen = {}

        def read(c):
            if c not in seen:
                seen[c] = ref[index, r, wide(c)]
            return seen[c]

        return read

    def first_pass(t, _):
        r = rows_of(t)
        for c in range(blocks):
            lift = 0.125 * ckpt[0, r, wide(c)]
            down = r0 - lift
            rise = r0 + lift
            for d in range(dirs):
                v = state[d, r, thin(c)]
                pa[d, r, wide(c)] = v * down
                qa[d, r, wide(c)] = v * rise
        return 0

    def advance(c, scale, base, ps, qs, d, p, q, b, a):
        here_p = ps[d](c)
        here_q = qs[d](c)
        return (
            scale * base
            + (upper(here_p, p[d, a, wide(c)]) + lower(q[d, b, wide(c)], here_q))
            + (right(here_p, ps[d](c + 1)) + left(qs[d](c - 1), here_q))
        )

    def second_pass(t, _):
        b, r, a = around(t)
        ps = [row_reader(pa, d, r) for d in range(dirs)]
        qs = [row_reader(qa, d, r) for d in range(dirs)]
        for c in range(blocks):
            lift = 0.125 * ckpt[1, r, wide(c)]
            down = r1 - lift
            rise = r1 + lift
            for d in range(dirs):
                w = advance(c, s0, state[d, r, thin(c)], ps, qs, d, pa, qa, b, a)
                w1[d, r, thin(c)] = w
                pb[d, r, wide(c)] = w * down
                qb[d, r, wide(c)] = w * rise
        return 0

    def third_pass(t, _):
        b, r, a = around(t)
        ps = [row_reader(pb, d, r) for d in range(dirs)]
        qs = [row_reader(qb, d, r) for d in range(dirs)]
        for c in range(blocks):
            weight = obs[r, thin(c)]
            for d in range(dirs):
                w = advance(c, s1, w1[d, r, thin(c)], ps, qs, d, pb, qb, b, a)
                pa[d, r, wide(c)] = weight * w
        return 0

    def pull(t, rate, scale, vel, adj, hist, q, emit):
        b, r, a = around(t)
        slopes = row_reader(ckpt, adj, r)
        readers = [row_reader(q, d, r) for d in range(dirs)]
        for c in range(blocks):
            lift = 0.125 * ckpt[vel, r, wide(c)]
            rise = rate + lift
            down = rate - lift
            here = slopes(c)
            slope = 0.125 * (
                (upper(here, ckpt[adj, a, wide(c)]) + right(here, slopes(c + 1)))
                - (lower(ckpt[adj, b, wide(c)], here) + left(slopes(c - 1), here))
            )
            for d in range(dirs):
                here = readers[d](c)
                plus = upper(here, q[d, a, wide(c)]) + right(here, readers[d](c + 1))
                minus = lower(q[d, b, wide(c)], here) + left(readers[d](c - 1), here)
                past = hist[d, r, thin(c)]
                emit(c, d, past, (scale * here + past * slope) + (rise * plus + down * minus))

    def fourth_pass(t, _):
        r = rows_of(t)

        def emit(c, d, past, value):
            qa[d, r, wide(c)] = value

        pull(t, r1, s1, 1, 3, w1, pa, emit)
        return 0

    half = tiles // 2

    def out_copy(part):
        span = pl.ds(part * half * TILE, half * TILE)
        return pltpu.make_async_copy(
            out.at[:, span], product_hbm.at[:, span], sems.at[part]
        )

    def fifth_pass(t, sums):
        sums = list(sums)
        o = rows_of(t - 1)

        def emit(c, d, past, value):
            value = value + prior[o, thin(c)] * past
            out[d, o, thin(c)] = value
            lot = d * SUMS + c % SUMS
            sums[lot] = sums[lot] + past * value

        pull(t, r0, s0, 0, 2, state, qa, emit)

        @pl.when(t == half)
        def _():
            out_copy(0).start()

        return tuple(sums)

    def close_edges(refs, at):
        for flag, t in ((0, 0), (1, tiles + 1)):

            @pl.when(meta_ref[EDGES + flag] == 0)
            def _():
                for ref in refs:
                    for d in range(dirs):
                        ref[d, pl.ds(t * TILE, TILE), at] = jnp.zeros((TILE, cols), jnp.float32)

    lax.fori_loop(0, tiles + 2, first_pass, 0)
    lax.fori_loop(0, tiles + 2, second_pass, 0)
    close_edges((pb, qb), middle)
    close_edges((w1,), pl.ds(0, cols))
    obs_copy.wait()
    lax.fori_loop(0, tiles + 2, third_pass, 0)
    close_edges((pa,), middle)
    lax.fori_loop(0, tiles + 2, fourth_pass, 0)
    close_edges((qa,), middle)
    prior_copy.wait()
    zero = jnp.zeros((TILE, LANES), jnp.float32)
    sums = lax.fori_loop(1, tiles + 1, fifth_pass, (zero,) * (SUMS * dirs))
    out_copy(1).start()
    for d in range(dirs):
        total = sums[d * SUMS]
        for lot in range(1, SUMS):
            total = total + sums[d * SUMS + lot]
        total = jnp.sum(total, axis=(0, 1), keepdims=True)
        curv_ref[pl.ds(d, 1), :] = jnp.broadcast_to(total, (1, LANES))
    out_copy(0).wait()
    out_copy(1).wait()


def stencil(meta, steps, diffusion, dirs, pieces, obs, prior, top, bottom, ctop, cbottom):
    count, rows, cols = dirs.shape
    ext = rows + 2 * TILE
    wide = cols + 2 * LANES
    vmem = pl.BlockSpec(memory_space=pltpu.VMEM)
    smem = pl.BlockSpec(memory_space=pltpu.SMEM)
    anywhere = pl.BlockSpec(memory_space=pl.ANY)
    f32 = jnp.float32
    return pl.pallas_call(
        stencil_kernel,
        out_shape=(
            jax.ShapeDtypeStruct(dirs.shape, f32),
            jax.ShapeDtypeStruct((count, 128), f32),
        ),
        in_specs=[smem] * 3 + [anywhere] * 7 + [vmem] * 4,
        out_specs=(anywhere, vmem),
        scratch_shapes=[
            pltpu.VMEM((count, ext, cols), f32),
            pltpu.VMEM((2 * STEPS, ext, wide), f32),
            pltpu.VMEM((ext, cols), f32),
            pltpu.VMEM((rows, cols), f32),
            pltpu.VMEM((count, ext, wide), f32),
            pltpu.VMEM((count, ext, wide), f32),
            pltpu.VMEM((count, ext, cols), f32),
            pltpu.VMEM((count, ext, wide), f32),
            pltpu.VMEM((count, ext, wide), f32),
            pltpu.VMEM((count, rows, cols), f32),
            pltpu.SemaphoreType.DMA((3 + len(pieces),)),
        ],
        compiler_params=pltpu.CompilerParams(vmem_limit_bytes=34 * 1024 * 1024),
    )(meta, steps, diffusion, dirs, *pieces, obs, prior, top, bottom, ctop, cbottom)


def per_device(directions, pool, owners, window_steps, diffusion, obs_weight, prior_diag):
    peers = lax.axis_size("space")
    groups = lax.axis_size("dir")
    slots, rows, cols = pool.shape
    rings = groups // RING
    quarter = rows // RING
    up = [(i, i + 1) for i in range(peers - 1)]
    down = [(j, i) for i, j in up]
    forward = [(r * RING + y, r * RING + (y + 1) % RING) for r in range(rings) for y in range(RING)]
    backward = [(j, i) for i, j in forward]
    swap = [(i, (i + RING) % groups) for i in range(groups)]

    smem = pl.BlockSpec(memory_space=pltpu.SMEM)
    vmem = pl.BlockSpec(memory_space=pltpu.VMEM)
    anywhere = pl.BlockSpec(memory_space=pl.ANY)
    small = pltpu.CompilerParams(vmem_limit_bytes=8 * 1024 * 1024)
    meta = pl.pallas_call(
        functools.partial(meta_kernel, slots),
        out_shape=jax.ShapeDtypeStruct((SHARED + 1,), jnp.int32),
        in_specs=[smem],
        out_specs=smem,
    )(owners)

    def scatter(width):
        def run(meta, pool, directions, obs_weight):
            parts = pl.pallas_call(
                quarters_kernel,
                out_shape=[jax.ShapeDtypeStruct((width, quarter, cols), pool.dtype)] * RING,
                in_specs=[smem, anywhere],
                out_specs=[vmem] * RING,
                scratch_shapes=[pltpu.SemaphoreType.DMA((RING,))],
                compiler_params=small,
            )(meta, pool)
            arrived = {(0, 0): parts[0]}
            for dx, dy in OFFSETS:
                pairs = [
                    (r * RING + y, (r + dx) % rings * RING + (y + dy) % RING)
                    for r in range(rings)
                    for y in range(RING)
                ]
                arrived[dx, dy] = lax.ppermute(parts[(dy + 2 * dx) % RING], "dir", pairs)
            arrived = [arrived[dx, dy] for dx in range(rings) for dy in range(RING)]
            first = jnp.concatenate([directions[:, :HALO], obs_weight[None, :HALO]], axis=0)
            last = jnp.concatenate([directions[:, -HALO:], obs_weight[None, -HALO:]], axis=0)
            before = lax.ppermute(last, "space", up)
            after = lax.ppermute(first, "space", down)
            own = pl.pallas_call(
                pick_kernel,
                out_shape=jax.ShapeDtypeStruct((2 * STEPS, quarter, cols), pool.dtype),
                in_specs=[smem] + [vmem] * groups,
                out_specs=vmem,
                scratch_shapes=[pltpu.SemaphoreType.DMA((2 * STEPS,))],
                compiler_params=small,
            )(meta, *arrived)
            return own, before, after

        return run

    own, top, bottom = lax.cond(
        meta[SHARED] > 0, scatter(slots), scatter(1), meta, pool, directions, obs_weight
    )
    across = lax.ppermute(own, "dir", swap)
    before = lax.ppermute(own, "dir", forward)
    after = lax.ppermute(own, "dir", backward)

    def holding(q, take):
        return jnp.where(
            meta[QUARTERS] == q,
            take(own),
            jnp.where(
                meta[QUARTERS + 1] == q,
                take(before),
                jnp.where(meta[QUARTERS + 2] == q, take(after), take(across)),
            ),
        )

    ctop = lax.ppermute(holding(RING - 1, lambda x: x[:, -HALO:]), "space", up)
    cbottom = lax.ppermute(holding(0, lambda x: x[:, :HALO]), "space", down)
    product, partial_sums = stencil(
        meta, window_steps, diffusion, directions, (own, before, after, across),
        obs_weight, prior_diag, top, bottom, ctop, cbottom,
    )
    spread = jnp.broadcast_to(partial_sums[None], (peers,) + partial_sums.shape)
    gathered = lax.all_to_all(spread, "space", 0, 0, tiled=True)
    summed = jnp.sum(gathered, axis=0)[:, 0]
    cells = directions.shape[1] * peers * directions.shape[2]
    return (product, summed / cells)


def solution(mesh):
    return jax.shard_map(
        per_device,
        mesh=mesh,
        in_specs=(
            P("dir", "space", None),
            P("dir", "space", None),
            P(),
            P(),
            P(),
            P("space", None),
            P("space", None),
        ),
        out_specs=(P("dir", "space", None), P("dir")),
        check_vma=False,
    )
```
